32 devices in a mesh: dp: 8 (over y, x, core), fsdp: 4 (over z).
Axes of the slice: x: 2, y: 2, z: 4, core: 2. Of those that a mesh axis runs over, the one named last changes fastest.
Arguments:
- inputs: bfloat16 [8, 512, 1024], P('dp', 'fsdp'), may hold values from -6 to 6
- gain_mixer: bfloat16 [1024], P(('dp', 'fsdp')), may hold values from 0.5 to 1.5
- weight_in: bfloat16 [1024, 3072], P(('dp', 'fsdp')), may hold values from -0.1875 to 0.1875
- conv_taps: bfloat16 [3, 1024], P(None, ('dp', 'fsdp')), may hold values from -3.5 to 3.5
- weight_out: bfloat16 [1024, 1024], P(('dp', 'fsdp')), may hold values from -0.1875 to 0.1875
- gain_ffn: bfloat16 [1024], P(('dp', 'fsdp')), may hold values from 0.5 to 1.5
- weight_gate: bfloat16 [1024, 4608], P(('dp', 'fsdp')), may hold values from -0.1875 to 0.1875
- weight_up: bfloat16 [1024, 4608], P(('dp', 'fsdp')), may hold values from -0.1875 to 0.1875
- weight_down: bfloat16 [4608, 1024], P(('dp', 'fsdp')), may hold values from -0.09375 to 0.09375
- cotangent: bfloat16 [8, 512, 1024], P('dp', 'fsdp'), may hold values from -6 to 6
Outputs:
- outputs: bfloat16 [8, 512, 1024], P('dp', 'fsdp')
- grad_inputs: float32 [8, 512, 1024], P('dp', 'fsdp')
- grad_gain_mixer: float32 [1024], P(('dp', 'fsdp'))
- grad_weight_in: float32 [1024, 3072], P(('dp', 'fsdp'))
- grad_conv_taps: float32 [3, 1024], P(None, ('dp', 'fsdp'))
- grad_weight_out: float32 [1024, 1024], P(('dp', 'fsdp'))
- grad_gain_ffn: float32 [1024], P(('dp', 'fsdp'))
- grad_weight_gate: float32 [1024, 4608], P(('dp', 'fsdp'))
- grad_weight_up: float32 [1024, 4608], P(('dp', 'fsdp'))
- grad_weight_down: float32 [4608, 1024], P(('dp', 'fsdp'))
The draws below stay inside these ranges and needn't reach their ends.
All inputs are finite; a program needn't handle non-finite values.
Results may differ from the reference program's by a relative error of at most 0.0088.
Values may be sent and summed in bfloat16 or wider, within the bound.
A program may use at most 192 MiB of HBM per device.

```python
import jax
import jax.numpy as jnp
from jax import lax

D = 1024
FF = 4608
KW = 3
LENGTH = 512
SEQS = 8


def spiked(array, key, source, target, shards_of, factor):
    owner, partner = [(jnp.arange(array.shape[position]) // (array.shape[position] // shards_of)).reshape([-1 if axis == position else 1 for axis in range(array.ndim)]) for position in (source, target)]
    chosen = jax.random.permutation(key, shards_of)[partner]
    strong = (owner == chosen) | (owner == (partner + shards_of // 2) % shards_of)
    return jnp.where(strong, factor * array, array)


def levels(key, dims, cuts, least, high):
    factor_of, own = 1.0, jax.random.fold_in(key, 6)
    for position, shards_of in cuts:
        heights = jnp.exp(jax.random.uniform(jax.random.fold_in(own, position), (shards_of,), jnp.float32, least / len(cuts), high / len(cuts)))
        factor_of = factor_of * jnp.repeat(heights, dims[position] // shards_of).reshape([-1 if axis == position else 1 for axis in range(len(dims))])
    return factor_of


def gaussian(key, shape, deviation, limit, split=(), held_as=jnp.bfloat16):
    factor_of = levels(key, shape, split, -0.22, 0.18) if split else 1.0
    values = jax.random.normal(key, shape, jnp.float32) * deviation * factor_of
    return jnp.minimum(jnp.maximum(values, -limit), limit).astype(held_as)


def noise_with(key, extent, scale, reach, cuts, heavy, held_as=jnp.bfloat16):
    values = scale * jax.random.normal(key, extent, jnp.float32)
    if cuts:
        values = values * levels(key, extent, cuts, -0.22, 0.18)
    return jnp.clip(spiked(values, jax.random.fold_in(key, 3), *heavy), -reach, reach).astype(held_as)


def setup_inputs(seed: int = 0) -> dict:
    key_of = jax.random.split(jax.random.key(seed), 11)
    return {
        "inputs": noise_with(key_of[0], (SEQS, LENGTH, D), 1.0, 6.0, ((0, 8), (1, 4)), (0, 2, 8, 2.0)),
        "gain_mixer": jnp.clip(1.0 + 0.1 * jax.random.normal(key_of[1], (D,), jnp.float32), 0.5, 1.5).astype(jnp.bfloat16),
        "weight_in": gaussian(key_of[2], (D, 3 * D), D ** -0.5, 0.1875, ((0, 32),)),
        "conv_taps": gaussian(key_of[3], (KW, D), KW ** -0.5, 3.5, ((1, 32),)),
        "weight_out": gaussian(key_of[4], (D, D), D ** -0.5, 0.1875, ((0, 32),)),
        "gain_ffn": jnp.clip(1.0 + 0.1 * jax.random.normal(key_of[5], (D,), jnp.float32), 0.5, 1.5).astype(jnp.bfloat16),
        "weight_gate": gaussian(key_of[6], (D, FF), D ** -0.5, 0.1875, ((0, 32),)),
        "weight_up": gaussian(key_of[7], (D, FF), D ** -0.5, 0.1875, ((0, 32),)),
        "weight_down": gaussian(key_of[8], (FF, D), FF ** -0.5, 0.09375, ((0, 32),)),
        "cotangent": gaussian(key_of[9], (SEQS, LENGTH, D), 1.0, 6.0, ((0, 8), (1, 4))),
    }


EPS = 1e-05

def product(left, right):
    return jnp.dot(left, right, preferred_element_type=jnp.float32)

def norm_forward(hidden, gain):
    scale = lax.rsqrt(lax.optimization_barrier(jnp.mean(hidden * hidden, axis=-1, keepdims=True)) + EPS)
    normed = hidden * scale
    return (normed, scale, normed * gain.astype(jnp.float32))

def norm_backward(dact, normed, scale, gain):
    dnormed = dact * gain.astype(jnp.float32)
    dhidden = scale * (dnormed - normed * lax.optimization_barrier(jnp.mean(dnormed * normed, axis=-1, keepdims=True)))
    return (dhidden, lax.optimization_barrier(jnp.sum(dact * normed, axis=0)))

def lagged(values, offset):
    zeros = jnp.zeros((offset, values.shape[1]), values.dtype)
    return jnp.concatenate([zeros, values[:values.shape[0] - offset]], axis=0)

def leading(values, offset):
    zeros = jnp.zeros((offset, values.shape[1]), values.dtype)
    return jnp.concatenate([values[offset:], zeros], axis=0)

def reference(inputs, gain_mixer, weight_in, conv_taps, weight_out, gain_ffn, weight_gate, weight_up, weight_down, cotangent):
    width = weight_out.shape[0]
    taps32 = conv_taps.astype(jnp.float32)

    def one_sequence(carry, pair):
        tokens, grad_out = pair
        hidden = tokens.astype(jnp.float32)
        normed1, scale1, pre1 = norm_forward(hidden, gain_mixer)
        act1 = pre1.astype(jnp.bfloat16)
        projected = product(act1, weight_in)
        bpart = projected[:, :width]
        cpart = projected[:, width:2 * width]
        xpart = projected[:, 2 * width:]
        gated = bpart * xpart
        conv = jnp.zeros_like(gated)
        for offset in range(KW):
            conv = conv + taps32[offset] * lagged(gated, offset)
        act2 = (cpart * conv).astype(jnp.bfloat16)
        resid = hidden + product(act2, weight_out)
        normed2, scale2, pre2 = norm_forward(resid, gain_ffn)
        act3 = pre2.astype(jnp.bfloat16)
        gate = product(act3, weight_gate)
        upval = product(act3, weight_up)
        sig = jax.nn.sigmoid(gate)
        act4 = (gate * sig * upval).astype(jnp.bfloat16)
        outputs = (resid + product(act4, weight_down)).astype(jnp.bfloat16)
        g_down = product(act4.T, grad_out)
        dact4 = product(grad_out, weight_down.T)
        dgate = (dact4 * upval * sig * (1.0 + gate * (1.0 - sig))).astype(jnp.bfloat16)
        dupval = (dact4 * gate * sig).astype(jnp.bfloat16)
        g_gate = product(act3.T, dgate)
        g_up = product(act3.T, dupval)
        dact3 = product(dgate, weight_gate.T) + product(dupval, weight_up.T)
        dnorm2, g_gain2 = norm_backward(dact3, normed2, scale2, gain_ffn)
        dresid = grad_out.astype(jnp.float32) + dnorm2
        dres16 = dresid.astype(jnp.bfloat16)
        g_out = product(act2.T, dres16)
        dact2 = product(dres16, weight_out.T)
        dcpart = dact2 * conv
        dconv = dact2 * cpart
        g_taps = jnp.stack([lax.optimization_barrier(jnp.sum(dconv * lagged(gated, offset), axis=0)) for offset in range(KW)], axis=0)
        dgated = jnp.zeros_like(dconv)
        for offset in range(KW):
            dgated = dgated + taps32[offset] * leading(dconv, offset)
        dproj = jnp.concatenate([dgated * xpart, dcpart, dgated * bpart], axis=1).astype(jnp.bfloat16)
        g_in = product(act1.T, dproj)
        dact1 = product(dproj, weight_in.T)
        dnorm1, g_gain1 = norm_backward(dact1, normed1, scale1, gain_mixer)
        grad_in = dresid + dnorm1
        terms = (g_gain1, g_in, g_taps, g_out, g_gain2, g_gate, g_up, g_down)
        carry = tuple((total + term for total, term in zip(carry, terms)))
        return (carry, (outputs, grad_in))
    start = (jnp.zeros(gain_mixer.shape, jnp.float32), jnp.zeros(weight_in.shape, jnp.float32), jnp.zeros(conv_taps.shape, jnp.float32), jnp.zeros(weight_out.shape, jnp.float32), jnp.zeros(gain_ffn.shape, jnp.float32), jnp.zeros(weight_gate.shape, jnp.float32), jnp.zeros(weight_up.shape, jnp.float32), jnp.zeros(weight_down.shape, jnp.float32))
    totals, stacked = lax.scan(one_sequence, start, (inputs, cotangent))
    outputs, grad_inputs = stacked
    return (outputs, grad_inputs, totals[0], totals[1], totals[2], totals[3], totals[4], totals[5], totals[6], totals[7])
```

```python
import jax
import jax.numpy as jnp
from jax import lax
from jax.sharding import PartitionSpec as P

KW = 3


EPS = 1e-05

GRAD = jnp.float32


def product(left, right):
    return jnp.dot(left, right, preferred_element_type=jnp.float32)


def product_tn(left, right):
    return lax.dot_general(
        left, right, (((0,), (0,)), ((), ())), preferred_element_type=jnp.float32
    )


def product_nt(left, right):
    return lax.dot_general(
        left, right, (((1,), (1,)), ((), ())), preferred_element_type=jnp.float32
    )


def norm_forward(hidden, gain):
    scale = lax.rsqrt(jnp.mean(hidden * hidden, axis=-1, keepdims=True) + EPS)
    normed = hidden * scale
    return (normed, scale, normed * gain.astype(jnp.float32))


def norm_backward(dact, normed, scale, gain):
    dnormed = dact * gain.astype(jnp.float32)
    dhidden = scale * (dnormed - normed * jnp.mean(dnormed * normed, axis=-1, keepdims=True))
    return (dhidden, jnp.sum(dact * normed, axis=0))


def lagged(values, offset):
    zeros = jnp.zeros((offset, values.shape[1]), values.dtype)
    return jnp.concatenate([zeros, values[: values.shape[0] - offset]], axis=0)


def leading(values, offset):
    zeros = jnp.zeros((offset, values.shape[1]), values.dtype)
    return jnp.concatenate([values[offset:], zeros], axis=0)


def whole_sequence(rows):
    return lax.all_gather(rows, "fsdp", axis=0, tiled=True)


def token_share(partial_value):
    fs_count = lax.axis_size("fsdp")
    rows, columns = partial_value.shape
    pieces = partial_value.astype(jnp.bfloat16).reshape(fs_count, rows // fs_count, columns)
    received = lax.all_to_all(pieces, "fsdp", split_axis=0, concat_axis=0, tiled=True)
    return jnp.sum(received.astype(jnp.float32), axis=0)


def column_blocks(shard, lead, dp_count, fs_count):
    rows, columns = shard.shape
    inner = columns // (lead * dp_count * fs_count)
    pieces = shard.reshape(rows, lead, dp_count, fs_count, inner).transpose(3, 0, 1, 2, 4)
    return pieces.reshape(fs_count, rows, lead * dp_count * inner)


def column_join(blocks, lead, dp_count, fs_count):
    _, rows, columns = blocks.shape
    inner = columns // (lead * dp_count)
    pieces = blocks.reshape(fs_count, rows, lead, dp_count, inner).transpose(1, 2, 3, 0, 4)
    return pieces.reshape(rows, lead * dp_count * fs_count * inner)


def exchange(blocks):
    return lax.all_to_all(blocks, "fsdp", split_axis=0, concat_axis=0, tiled=True)


def gather_dp(rows):
    return lax.all_gather(rows, "dp", axis=0, tiled=True)


def reduce_dp(partial_grad):
    return lax.psum_scatter(partial_grad, "dp", scatter_dimension=0, tiled=True)


def split_features(
    inputs,
    gain_mixer,
    weight_in,
    conv_taps,
    weight_out,
    gain_ffn,
    weight_gate,
    weight_up,
    weight_down,
    cotangent,
):
    dp_count = lax.axis_size("dp")
    fs_count = lax.axis_size("fsdp")
    width = weight_out.shape[1]
    part = weight_out.shape[0]
    quarter = dp_count * part
    hid = dp_count * weight_down.shape[0]

    x_all = whole_sequence(inputs[0])
    small = jnp.concatenate([gain_mixer[None], gain_ffn[None], conv_taps], axis=0)
    small_all = lax.all_gather(small, ("dp", "fsdp"), axis=1, tiled=True)
    gain1, gain2 = small_all[0], small_all[1]
    taps32 = lax.dynamic_index_in_dim(
        small_all[2:].reshape(KW, dp_count, fs_count, part),
        lax.axis_index("fsdp"),
        axis=2,
        keepdims=False,
    ).reshape(KW, quarter).astype(jnp.float32)

    in_blocks = exchange(column_blocks(weight_in, 3, dp_count, fs_count))
    gu_blocks = exchange(
        jnp.concatenate(
            [
                column_blocks(weight_gate, 1, dp_count, fs_count),
                column_blocks(weight_up, 1, dp_count, fs_count),
            ],
            axis=2,
        )
    )
    in_cols = gather_dp(in_blocks.reshape(fs_count * part, 3 * quarter))
    out_rows = gather_dp(weight_out)
    gu_cols = gather_dp(gu_blocks.reshape(fs_count * part, 2 * hid))
    down_rows = gather_dp(weight_down)
    grad_out = cotangent[0]
    grad_all = whole_sequence(grad_out)

    _, _, pre1_all = norm_forward(x_all.astype(jnp.float32), gain1)
    act1_all = pre1_all.astype(jnp.bfloat16)
    projected = product(act1_all, in_cols)
    bpart = projected[:, :quarter]
    cpart = projected[:, quarter : 2 * quarter]
    xpart = projected[:, 2 * quarter :]
    gated = bpart * xpart
    lagged_rows = [lagged(gated, offset) for offset in range(KW)]
    conv = taps32[0] * lagged_rows[0]
    for offset in range(1, KW):
        conv = conv + taps32[offset] * lagged_rows[offset]
    act2 = (cpart * conv).astype(jnp.bfloat16)
    hidden = inputs[0].astype(jnp.float32)
    normed1, scale1, _ = norm_forward(hidden, gain1)
    resid = hidden + token_share(product(act2, out_rows))
    normed2, scale2, pre2 = norm_forward(resid, gain2)
    act3_all = whole_sequence(pre2.astype(jnp.bfloat16))
    gate_up = product(act3_all, gu_cols)
    gate, upval = gate_up[:, :hid], gate_up[:, hid:]
    sig = jax.nn.sigmoid(gate)
    act4 = (gate * sig * upval).astype(jnp.bfloat16)
    dact4 = product_nt(grad_all, down_rows)
    dgate = (dact4 * upval * sig * (1.0 + gate * (1.0 - sig))).astype(jnp.bfloat16)
    dupval = (dact4 * gate * sig).astype(jnp.bfloat16)
    dgu = jnp.concatenate([dgate, dupval], axis=1)
    dact3 = token_share(product_nt(dgu, gu_cols))
    outputs = (resid + token_share(product(act4, down_rows))).astype(jnp.bfloat16)
    g_gu = reduce_dp(product_tn(act3_all, dgu).astype(GRAD))
    g_down = reduce_dp(product_tn(act4, grad_all).astype(GRAD))
    dnorm2, g_gain2 = norm_backward(dact3, normed2, scale2, gain2)
    dresid = grad_out.astype(jnp.float32) + dnorm2
    dres_all = whole_sequence(dresid.astype(jnp.bfloat16))
    dact2 = product_nt(dres_all, out_rows)
    dcpart = dact2 * conv
    dconv = dact2 * cpart
    g_taps = jnp.stack(
        [jnp.sum(dconv * lagged_rows[offset], axis=0) for offset in range(KW)], axis=0
    )
    dgated = taps32[0] * dconv
    for offset in range(1, KW):
        dgated = dgated + taps32[offset] * leading(dconv, offset)
    dproj = jnp.concatenate([dgated * xpart, dcpart, dgated * bpart], axis=1).astype(jnp.bfloat16)
    dact1 = token_share(product_nt(dproj, in_cols))
    g_in = reduce_dp(product_tn(act1_all, dproj).astype(GRAD))
    g_out = reduce_dp(product_tn(act2, dres_all).astype(GRAD))
    dnorm1, g_gain1 = norm_backward(dact1, normed1, scale1, gain1)
    grad_inputs = dresid + dnorm1

    g_gu_owned = exchange(g_gu.reshape(fs_count, part, 2 * hid).astype(jnp.bfloat16)).astype(jnp.float32)
    g_in_owned = exchange(g_in.reshape(fs_count, part, 3 * quarter).astype(jnp.bfloat16)).astype(jnp.float32)
    own_column = (jnp.arange(fs_count) == lax.axis_index("fsdp"))[None, None, :, None]
    taps_spread = jnp.where(own_column, g_taps.reshape(KW, dp_count, 1, part), 0.0).reshape(KW, width)
    small_owned = lax.psum_scatter(
        jnp.concatenate([g_gain1[None], g_gain2[None], taps_spread], axis=0),
        ("dp", "fsdp"),
        scatter_dimension=1,
        tiled=True,
    )
    return (
        outputs[None],
        grad_inputs[None],
        small_owned[0],
        column_join(g_in_owned, 3, dp_count, fs_count),
        small_owned[2:],
        g_out.astype(jnp.float32),
        small_owned[1],
        column_join(g_gu_owned[:, :, :hid], 1, dp_count, fs_count),
        column_join(g_gu_owned[:, :, hid:], 1, dp_count, fs_count),
        g_down.astype(jnp.float32),
    )


def on_device(
    inputs,
    gain_mixer,
    weight_in,
    conv_taps,
    weight_out,
    gain_ffn,
    weight_gate,
    weight_up,
    weight_down,
    cotangent,
):
    return split_features(
        inputs,
        gain_mixer,
        weight_in,
        conv_taps,
        weight_out,
        gain_ffn,
        weight_gate,
        weight_up,
        weight_down,
        cotangent,
    )


def solution(mesh):
    in_specs = (
        P("dp", "fsdp", None),
        P(("dp", "fsdp")),
        P(("dp", "fsdp"), None),
        P(None, ("dp", "fsdp")),
        P(("dp", "fsdp"), None),
        P(("dp", "fsdp")),
        P(("dp", "fsdp"), None),
        P(("dp", "fsdp"), None),
        P(("dp", "fsdp"), None),
        P("dp", "fsdp", None),
    )
    out_specs = (
        P("dp", "fsdp", None),
        P("dp", "fsdp", None),
        P(("dp", "fsdp")),
        P(("dp", "fsdp"), None),
        P(None, ("dp", "fsdp")),
        P(("dp", "fsdp"), None),
        P(("dp", "fsdp")),
        P(("dp", "fsdp"), None),
        P(("dp", "fsdp"), None),
        P(("dp", "fsdp"), None),
    )
    return jax.shard_map(
        on_device, mesh=mesh, in_specs=in_specs, out_specs=out_specs, check_vma=False
    )
```

```python
import functools

import jax
import jax.numpy as jnp
from jax import lax
from jax.experimental import pallas as pl
from jax.experimental.pallas import tpu as pltpu
from jax.sharding import PartitionSpec as P

KW = 3


EPS = 1e-05

CORES = 2
MESH = pl.DeviceIdType.MESH


def product(left, right):
    return jnp.dot(left, right, preferred_element_type=jnp.float32)


def product_tn(left, right):
    return lax.dot_general(
        left, right, (((0,), (0,)), ((), ())), preferred_element_type=jnp.float32
    )


def product_nt(left, right):
    return lax.dot_general(
        left, right, (((1,), (1,)), ((), ())), preferred_element_type=jnp.float32
    )


def norm_forward(hidden, gain):
    scale = lax.rsqrt(jnp.mean(hidden * hidden, axis=-1, keepdims=True) + EPS)
    normed = hidden * scale
    return (normed, scale, normed * gain.astype(jnp.float32))


def norm_backward(dact, normed, scale, gain):
    dnormed = dact * gain.astype(jnp.float32)
    dhidden = scale * (dnormed - normed * jnp.mean(dnormed * normed, axis=-1, keepdims=True))
    return (dhidden, jnp.sum(dact * normed, axis=0))


def lagged(values, offset):
    zeros = jnp.zeros((offset, values.shape[1]), values.dtype)
    return jnp.concatenate([zeros, values[: values.shape[0] - offset]], axis=0)


def leading(values, offset):
    zeros = jnp.zeros((offset, values.shape[1]), values.dtype)
    return jnp.concatenate([values[offset:], zeros], axis=0)


def whole_sequence(rows):
    return lax.all_gather(rows, "fsdp", axis=0, tiled=True)


def token_share(partial_value):
    fs_count = lax.axis_size("fsdp")
    rows, columns = partial_value.shape
    pieces = partial_value.astype(jnp.bfloat16).reshape(fs_count, rows // fs_count, columns)
    received = lax.all_to_all(pieces, "fsdp", split_axis=0, concat_axis=0, tiled=True)
    return jnp.sum(received.astype(jnp.float32), axis=0)


def column_blocks(shard, lead, dp_count, fs_count):
    rows, columns = shard.shape
    inner = columns // (lead * dp_count * fs_count)
    pieces = shard.reshape(rows, lead, dp_count, fs_count, inner).transpose(3, 0, 1, 2, 4)
    return pieces.reshape(fs_count, rows, lead * dp_count * inner)


def column_join(blocks, lead, dp_count, fs_count):
    _, rows, columns = blocks.shape
    inner = columns // (lead * dp_count)
    pieces = blocks.reshape(fs_count, rows, lead, dp_count, inner).transpose(1, 2, 3, 0, 4)
    return pieces.reshape(rows, lead * dp_count * fs_count * inner)


def exchange(blocks):
    return lax.all_to_all(blocks, "fsdp", split_axis=0, concat_axis=0, tiled=True)


def greet(peers):
    barrier = pltpu.get_barrier_semaphore()
    for peer in peers:
        pl.semaphore_signal(barrier, inc=1, device_id=peer, device_id_type=MESH)
    pl.semaphore_wait(barrier, len(peers))


def push(src, dst, sends, recvs, index, peer):
    copy = pltpu.make_async_remote_copy(
        src_ref=src,
        dst_ref=dst,
        send_sem=sends.at[index],
        recv_sem=recvs.at[index],
        device_id=peer,
        device_id_type=MESH,
    )
    copy.start()
    return copy


def place():
    dp, fs = lax.axis_index("dp"), lax.axis_index("fsdp")
    pair, core = dp // CORES, lax.rem(dp, CORES)
    return dp, fs, pair, core, (pair * CORES + 1 - core, fs)


def gather_kernel(
    pairs, fs_count,
    x_ref, cot_ref, small_ref, in_ref, gu_ref, out_ref, down_ref,
    x_all, cot_all, small_all, in_all, gu_all, out_all, down_all,
    local_sem, z_send, z_recv, p_send, p_recv, c_send, c_recv,
):
    dp, fs, pair, core, partner = place()
    z_peers = [(dp, lax.rem(fs + o, fs_count)) for o in range(1, fs_count)]
    p_peers = [(lax.rem(pair + o, pairs) * CORES + core, fs) for o in range(1, pairs)]
    p_from = [lax.rem(pair + pairs - o, pairs) * CORES + core for o in range(1, pairs)]
    greet(z_peers + p_peers + [partner])
    spread = [small_all, in_all, gu_all, out_all, down_all]

    across = [[None] * len(p_peers) for _ in spread]
    twins = [[None] * pairs for _ in spread]

    def spread_own(kind, src):
        dst = spread[kind].at[dp]
        for o, peer in enumerate(p_peers):
            across[kind][o] = push(src, dst, p_send, p_recv, (kind, o), peer)
        twins[kind][0] = push(src, dst, c_send, c_recv, (kind, 0), partner)

    along = [[], [], [], [], []]
    for o, peer in enumerate(z_peers):
        to = peer[1]
        along[0].append(push(small_ref, small_all.at[dp, fs], z_send, z_recv, (0, o), peer))
        along[1].append(push(in_ref.at[to], in_all.at[dp, fs], z_send, z_recv, (1, o), peer))
    for o, peer in enumerate(z_peers):
        to = peer[1]
        along[2].append(push(gu_ref.at[to], gu_all.at[dp, fs], z_send, z_recv, (2, o), peer))
    for o, peer in enumerate(z_peers):
        along[3].append(push(x_ref, x_all.at[fs], z_send, z_recv, (3, o), peer))
    for o, peer in enumerate(z_peers):
        along[4].append(push(cot_ref, cot_all.at[fs], z_send, z_recv, (4, o), peer))
    spread_own(3, out_ref)
    spread_own(4, down_ref)
    local = []
    for index, (src, dst) in enumerate(
        [
            (small_ref, small_all.at[dp, fs]),
            (in_ref.at[fs], in_all.at[dp, fs]),
            (gu_ref.at[fs], gu_all.at[dp, fs]),
            (x_ref, x_all.at[fs]),
            (cot_ref, cot_all.at[fs]),
            (out_ref, out_all.at[dp]),
            (down_ref, down_all.at[dp]),
        ]
    ):
        copy = pltpu.make_async_copy(src, dst, local_sem.at[index])
        copy.start()
        local.append(copy)
    for kind in range(3):
        local[kind].wait()
        for copy in along[kind]:
            copy.wait_recv()
        spread_own(kind, spread[kind].at[dp])
    for kind in (3, 0, 1, 4, 2):
        for o, source in enumerate(p_from):
            across[kind][o].wait_recv()
            block = spread[kind].at[source]
            twins[kind][o + 1] = push(block, block, c_send, c_recv, (kind, o + 1), partner)
    for copy in local[3:]:
        copy.wait()
    for copy in along[3] + along[4]:
        copy.wait_recv()
    for row in along + across:
        for copy in row:
            copy.wait_send()
    for row in twins:
        for copy in row:
            copy.wait()


def gather_all(x, cot, small, in_blocks, gu_blocks, out_shard, down_shard):
    dp_count, fs_count = lax.axis_size("dp"), lax.axis_size("fsdp")
    pairs = dp_count // CORES
    arrays = (x, cot, small, in_blocks, gu_blocks, out_shard, down_shard)
    shapes = (
        (fs_count,) + x.shape,
        (fs_count,) + cot.shape,
        (dp_count, fs_count) + small.shape,
        (dp_count,) + in_blocks.shape,
        (dp_count,) + gu_blocks.shape,
        (dp_count,) + out_shard.shape,
        (dp_count,) + down_shard.shape,
    )
    return pl.pallas_call(
        functools.partial(gather_kernel, pairs, fs_count),
        out_shape=[jax.ShapeDtypeStruct(shape, x.dtype) for shape in shapes],
        in_specs=[pl.BlockSpec(memory_space=pltpu.VMEM)] * len(arrays),
        out_specs=[pl.BlockSpec(memory_space=pl.ANY)] * len(shapes),
        scratch_shapes=[
            pltpu.SemaphoreType.DMA((7,)),
            pltpu.SemaphoreType.DMA((5, fs_count - 1)),
            pltpu.SemaphoreType.DMA((5, fs_count - 1)),
            pltpu.SemaphoreType.DMA((5, pairs - 1)),
            pltpu.SemaphoreType.DMA((5, pairs - 1)),
            pltpu.SemaphoreType.DMA((5, pairs)),
            pltpu.SemaphoreType.DMA((5, pairs)),
        ],
        compiler_params=pltpu.CompilerParams(collective_id=0, has_side_effects=True),
        name="gather_all",
    )(*arrays)


def twin_kernel(count, pairs, *refs):
    partials, received = refs[:count], refs[count : 2 * count]
    sends, recvs = refs[2 * count :]
    _, _, _, core, partner = place()
    greet([partner])
    copies = [
        push(partial.at[j, 1 - core], landed.at[j], sends, recvs, (k, j), partner)
        for k, (partial, landed) in enumerate(zip(partials, received))
        for j in range(pairs)
    ]
    for copy in copies:
        copy.wait()


def pair_kernel(count, pairs, *refs):
    partials, received = refs[:count], refs[count : 2 * count]
    sends, recvs = refs[2 * count :]
    _, fs, pair, core, _ = place()
    targets = [lax.rem(pair + o, pairs) for o in range(1, pairs)]
    peers = [(to * CORES + core, fs) for to in targets]
    greet(peers)
    copies = [
        push(partial.at[to], landed.at[o], sends, recvs, (k, o), peer)
        for k, (partial, landed) in enumerate(zip(partials, received))
        for o, (to, peer) in enumerate(zip(targets, peers))
    ]
    for copy in copies:
        copy.wait()


def exchange_call(kernel, partials, slots, collective_id, name):
    count = len(partials)
    pairs = lax.axis_size("dp") // CORES
    return pl.pallas_call(
        functools.partial(kernel, count, pairs),
        out_shape=[jax.ShapeDtypeStruct((slots,) + p.shape[-2:], p.dtype) for p in partials],
        in_specs=[pl.BlockSpec(memory_space=pl.ANY)] * count,
        out_specs=[pl.BlockSpec(memory_space=pl.ANY)] * count,
        scratch_shapes=[pltpu.SemaphoreType.DMA((count, slots))] * 2,
        compiler_params=pltpu.CompilerParams(collective_id=collective_id, has_side_effects=True),
        name=name,
    )(*partials)


def reduce_all(partials):
    dp_count = lax.axis_size("dp")
    pairs = dp_count // CORES
    dp = lax.axis_index("dp")
    core, pair = lax.rem(dp, CORES), dp // CORES
    split = [
        p.astype(jnp.bfloat16).reshape(pairs, CORES, p.shape[0] // dp_count, p.shape[1])
        for p in partials
    ]
    landed = exchange_call(twin_kernel, split, pairs, 1, "twin_exchange")
    chip = [
        (
            lax.dynamic_index_in_dim(p, core, axis=1, keepdims=False).astype(jnp.float32)
            + r.astype(jnp.float32)
        ).astype(jnp.bfloat16)
        for p, r in zip(split, landed)
    ]
    others = exchange_call(pair_kernel, chip, pairs - 1, 2, "pair_exchange")
    return [
        lax.dynamic_index_in_dim(p, pair, axis=0, keepdims=False).astype(jnp.float32)
        + jnp.sum(r.astype(jnp.float32), axis=0)
        for p, r in zip(chip, others)
    ]


def split_features(
    inputs,
    gain_mixer,
    weight_in,
    conv_taps,
    weight_out,
    gain_ffn,
    weight_gate,
    weight_up,
    weight_down,
    cotangent,
):
    dp_count = lax.axis_size("dp")
    fs_count = lax.axis_size("fsdp")
    width = weight_out.shape[1]
    part = weight_out.shape[0]
    quarter = dp_count * part
    hid = dp_count * weight_down.shape[0]

    small = jnp.concatenate([gain_mixer[None], gain_ffn[None], conv_taps], axis=0)
    lanes = max(128, part)
    small = jnp.pad(small, ((0, 8 - small.shape[0]), (0, lanes - part)))
    gu_blocks = jnp.concatenate(
        [
            column_blocks(weight_gate, 1, dp_count, fs_count),
            column_blocks(weight_up, 1, dp_count, fs_count),
        ],
        axis=2,
    )
    grad_out = cotangent[0]
    x_all, grad_all, small_all, in_cols, gu_cols, out_rows, down_rows = gather_all(
        inputs[0],
        grad_out,
        small,
        column_blocks(weight_in, 3, dp_count, fs_count),
        gu_blocks,
        weight_out,
        weight_down,
    )
    x_all = x_all.reshape(-1, width)
    grad_all = grad_all.reshape(-1, width)
    in_cols = in_cols.reshape(width, 3 * quarter)
    gu_cols = gu_cols.reshape(width, 2 * hid)
    out_rows = out_rows.reshape(quarter, width)
    down_rows = down_rows.reshape(hid, width)
    small_all = small_all[:, :, : KW + 2, :part]
    gain1 = small_all[:, :, 0].reshape(width)
    gain2 = small_all[:, :, 1].reshape(width)
    taps32 = (
        lax.dynamic_index_in_dim(small_all, lax.axis_index("fsdp"), axis=1, keepdims=False)[:, 2:]
        .transpose(1, 0, 2)
        .reshape(KW, quarter)
        .astype(jnp.float32)
    )

    _, _, pre1_all = norm_forward(x_all.astype(jnp.float32), gain1)
    act1_all = pre1_all.astype(jnp.bfloat16)
    projected = product(act1_all, in_cols)
    bpart = projected[:, :quarter]
    cpart = projected[:, quarter : 2 * quarter]
    xpart = projected[:, 2 * quarter :]
    gated = bpart * xpart
    lagged_rows = [lagged(gated, offset) for offset in range(KW)]
    conv = taps32[0] * lagged_rows[0]
    for offset in range(1, KW):
        conv = conv + taps32[offset] * lagged_rows[offset]
    act2 = (cpart * conv).astype(jnp.bfloat16)
    hidden = inputs[0].astype(jnp.float32)
    normed1, scale1, _ = norm_forward(hidden, gain1)
    resid = hidden + token_share(product(act2, out_rows))
    normed2, scale2, pre2 = norm_forward(resid, gain2)
    act3_all = whole_sequence(pre2.astype(jnp.bfloat16))
    gate_up = product(act3_all, gu_cols)
    gate, upval = gate_up[:, :hid], gate_up[:, hid:]
    sig = jax.nn.sigmoid(gate)
    act4 = (gate * sig * upval).astype(jnp.bfloat16)
    dact4 = product_nt(grad_all, down_rows)
    dgate = (dact4 * upval * sig * (1.0 + gate * (1.0 - sig))).astype(jnp.bfloat16)
    dupval = (dact4 * gate * sig).astype(jnp.bfloat16)
    dgu = jnp.concatenate([dgate, dupval], axis=1)
    dact3 = token_share(product_nt(dgu, gu_cols))
    outputs = (resid + token_share(product(act4, down_rows))).astype(jnp.bfloat16)
    dnorm2, g_gain2 = norm_backward(dact3, normed2, scale2, gain2)
    dresid = grad_out.astype(jnp.float32) + dnorm2
    dres_all = whole_sequence(dresid.astype(jnp.bfloat16))
    dact2 = product_nt(dres_all, out_rows)
    dcpart = dact2 * conv
    dconv = dact2 * cpart
    g_taps = jnp.stack(
        [jnp.sum(dconv * lagged_rows[offset], axis=0) for offset in range(KW)], axis=0
    )
    dgated = taps32[0] * dconv
    for offset in range(1, KW):
        dgated = dgated + taps32[offset] * leading(dconv, offset)
    dproj = jnp.concatenate([dgated * xpart, dcpart, dgated * bpart], axis=1).astype(jnp.bfloat16)
    dact1 = token_share(product_nt(dproj, in_cols))
    g_gu, g_down, g_in, g_out = reduce_all(
        [
            product_tn(act3_all, dgu),
            product_tn(act4, grad_all),
            product_tn(act1_all, dproj),
            product_tn(act2, dres_all),
        ]
    )
    dnorm1, g_gain1 = norm_backward(dact1, normed1, scale1, gain1)
    grad_inputs = dresid + dnorm1

    moved = jnp.concatenate([g_in, g_gu], axis=1).astype(jnp.bfloat16)
    moved = exchange(moved.reshape(fs_count, part, 3 * quarter + 2 * hid)).astype(jnp.float32)
    g_in_owned = moved[:, :, : 3 * quarter]
    g_gu_owned = moved[:, :, 3 * quarter :]
    own_column = (jnp.arange(fs_count) == lax.axis_index("fsdp"))[None, None, :, None]
    taps_spread = jnp.where(own_column, g_taps.reshape(KW, dp_count, 1, part), 0.0).reshape(KW, width)
    small_owned = lax.psum_scatter(
        jnp.concatenate([g_gain1[None], g_gain2[None], taps_spread], axis=0),
        ("dp", "fsdp"),
        scatter_dimension=1,
        tiled=True,
    )
    return (
        outputs[None],
        grad_inputs[None],
        small_owned[0],
        column_join(g_in_owned, 3, dp_count, fs_count),
        small_owned[2:],
        g_out,
        small_owned[1],
        column_join(g_gu_owned[:, :, :hid], 1, dp_count, fs_count),
        column_join(g_gu_owned[:, :, hid:], 1, dp_count, fs_count),
        g_down,
    )


def on_device(
    inputs,
    gain_mixer,
    weight_in,
    conv_taps,
    weight_out,
    gain_ffn,
    weight_gate,
    weight_up,
    weight_down,
    cotangent,
):
    return split_features(
        inputs,
        gain_mixer,
        weight_in,
        conv_taps,
        weight_out,
        gain_ffn,
        weight_gate,
        weight_up,
        weight_down,
        cotangent,
    )


def solution(mesh):
    in_specs = (
        P("dp", "fsdp", None),
        P(("dp", "fsdp")),
        P(("dp", "fsdp"), None),
        P(None, ("dp", "fsdp")),
        P(("dp", "fsdp"), None),
        P(("dp", "fsdp")),
        P(("dp", "fsdp"), None),
        P(("dp", "fsdp"), None),
        P(("dp", "fsdp"), None),
        P("dp", "fsdp", None),
    )
    out_specs = (
        P("dp", "fsdp", None),
        P("dp", "fsdp", None),
        P(("dp", "fsdp")),
        P(("dp", "fsdp"), None),
        P(None, ("dp", "fsdp")),
        P(("dp", "fsdp"), None),
        P(("dp", "fsdp")),
        P(("dp", "fsdp"), None),
        P(("dp", "fsdp"), None),
        P(("dp", "fsdp"), None),
    )
    return jax.shard_map(
        on_device, mesh=mesh, in_specs=in_specs, out_specs=out_specs, check_vma=False
    )
```

```python
import functools

import jax
import jax.numpy as jnp
from jax import lax
from jax.experimental import pallas as pl
from jax.experimental.pallas import tpu as pltpu
from jax.sharding import PartitionSpec as P

KW = 3


EPS = 1e-05

CORES = 2
MESH = pl.DeviceIdType.MESH


def product(left, right):
    return jnp.dot(left, right, preferred_element_type=jnp.float32)


def product_tn(left, right):
    return lax.dot_general(
        left, right, (((0,), (0,)), ((), ())), preferred_element_type=jnp.float32
    )


def product_nt(left, right):
    return lax.dot_general(
        left, right, (((1,), (1,)), ((), ())), preferred_element_type=jnp.float32
    )


def norm_forward(hidden, gain):
    scale = lax.rsqrt(jnp.mean(hidden * hidden, axis=-1, keepdims=True) + EPS)
    normed = hidden * scale
    return (normed, scale, normed * gain.astype(jnp.float32))


def norm_backward(dact, normed, scale, gain):
    dnormed = dact * gain.astype(jnp.float32)
    dhidden = scale * (dnormed - normed * jnp.mean(dnormed * normed, axis=-1, keepdims=True))
    return (dhidden, jnp.sum(dact * normed, axis=0))


def lagged(values, offset):
    zeros = jnp.zeros((offset, values.shape[1]), values.dtype)
    return jnp.concatenate([zeros, values[: values.shape[0] - offset]], axis=0)


def leading(values, offset):
    zeros = jnp.zeros((offset, values.shape[1]), values.dtype)
    return jnp.concatenate([values[offset:], zeros], axis=0)


def column_blocks(shard, lead, dp_count, fs_count):
    rows, columns = shard.shape
    inner = columns // (lead * dp_count * fs_count)
    pieces = shard.reshape(rows, lead, dp_count, fs_count, inner).transpose(3, 0, 1, 2, 4)
    return pieces.reshape(fs_count, rows, lead * dp_count * inner)


def column_join(blocks, lead, dp_count, fs_count):
    _, rows, columns = blocks.shape
    inner = columns // (lead * dp_count)
    pieces = blocks.reshape(fs_count, rows, lead, dp_count, inner).transpose(1, 2, 3, 0, 4)
    return pieces.reshape(rows, lead * dp_count * fs_count * inner)


def greet(peers):
    barrier = pltpu.get_barrier_semaphore()
    for peer in peers:
        pl.semaphore_signal(barrier, inc=1, device_id=peer, device_id_type=MESH)
    pl.semaphore_wait(barrier, len(peers))


def push(src, dst, sends, recvs, index, peer):
    copy = pltpu.make_async_remote_copy(
        src_ref=src,
        dst_ref=dst,
        send_sem=sends.at[index],
        recv_sem=recvs.at[index],
        device_id=peer,
        device_id_type=MESH,
    )
    copy.start()
    return copy


def place():
    dp, fs = lax.axis_index("dp"), lax.axis_index("fsdp")
    pair, core = dp // CORES, lax.rem(dp, CORES)
    return dp, fs, pair, core, (pair * CORES + 1 - core, fs)


def gather_kernel(
    pairs, fs_count,
    x_ref, cot_ref, small_ref, in_ref, gu_ref, out_ref, down_ref,
    x_all, cot_all, small_all, in_all, gu_all, out_all, down_all,
    local_sem, z_send, z_recv, p_send, p_recv, c_send, c_recv,
):
    dp, fs, pair, core, partner = place()
    z_peers = [(dp, lax.rem(fs + o, fs_count)) for o in range(1, fs_count)]
    p_peers = [(lax.rem(pair + o, pairs) * CORES + core, fs) for o in range(1, pairs)]
    p_from = [lax.rem(pair + pairs - o, pairs) * CORES + core for o in range(1, pairs)]
    greet(z_peers + p_peers + [partner])
    spread = [small_all, in_all, gu_all, out_all, down_all]

    across = [[None] * len(p_peers) for _ in spread]
    twins = [[None] * pairs for _ in spread]

    def spread_own(kind, src):
        dst = spread[kind].at[dp]
        for o, peer in enumerate(p_peers):
            across[kind][o] = push(src, dst, p_send, p_recv, (kind, o), peer)
        twins[kind][0] = push(src, dst, c_send, c_recv, (kind, 0), partner)

    along = [[], [], [], [], []]
    for o, peer in enumerate(z_peers):
        to = peer[1]
        along[0].append(push(small_ref, small_all.at[dp, fs], z_send, z_recv, (0, o), peer))
        along[1].append(push(in_ref.at[to], in_all.at[dp, fs], z_send, z_recv, (1, o), peer))
    for o, peer in enumerate(z_peers):
        to = peer[1]
        along[2].append(push(gu_ref.at[to], gu_all.at[dp, fs], z_send, z_recv, (2, o), peer))
    for o, peer in enumerate(z_peers):
        along[3].append(push(x_ref, x_all.at[fs], z_send, z_recv, (3, o), peer))
    for o, peer in enumerate(z_peers):
        along[4].append(push(cot_ref, cot_all.at[fs], z_send, z_recv, (4, o), peer))
    spread_own(3, out_ref)
    spread_own(4, down_ref)
    local = []
    for index, (src, dst) in enumerate(
        [
            (small_ref, small_all.at[dp, fs]),
            (in_ref.at[fs], in_all.at[dp, fs]),
            (gu_ref.at[fs], gu_all.at[dp, fs]),
            (x_ref, x_all.at[fs]),
            (cot_ref, cot_all.at[fs]),
            (out_ref, out_all.at[dp]),
            (down_ref, down_all.at[dp]),
        ]
    ):
        copy = pltpu.make_async_copy(src, dst, local_sem.at[index])
        copy.start()
        local.append(copy)
    for kind in range(3):
        local[kind].wait()
        for copy in along[kind]:
            copy.wait_recv()
        spread_own(kind, spread[kind].at[dp])
    for kind in (3, 0, 1, 4, 2):
        for o, source in enumerate(p_from):
            across[kind][o].wait_recv()
            block = spread[kind].at[source]
            twins[kind][o + 1] = push(block, block, c_send, c_recv, (kind, o + 1), partner)
    for copy in local[3:]:
        copy.wait()
    for copy in along[3] + along[4]:
        copy.wait_recv()
    for row in along + across:
        for copy in row:
            copy.wait_send()
    for row in twins:
        for copy in row:
            copy.wait()


def gather_all(x, cot, small, in_blocks, gu_blocks, out_shard, down_shard):
    dp_count, fs_count = lax.axis_size("dp"), lax.axis_size("fsdp")
    pairs = dp_count // CORES
    arrays = (x, cot, small, in_blocks, gu_blocks, out_shard, down_shard)
    shapes = (
        (fs_count,) + x.shape,
        (fs_count,) + cot.shape,
        (dp_count, fs_count) + small.shape,
        (dp_count,) + in_blocks.shape,
        (dp_count,) + gu_blocks.shape,
        (dp_count,) + out_shard.shape,
        (dp_count,) + down_shard.shape,
    )
    return pl.pallas_call(
        functools.partial(gather_kernel, pairs, fs_count),
        out_shape=[jax.ShapeDtypeStruct(shape, x.dtype) for shape in shapes],
        in_specs=[pl.BlockSpec(memory_space=pltpu.VMEM)] * len(arrays),
        out_specs=[pl.BlockSpec(memory_space=pl.ANY)] * len(shapes),
        scratch_shapes=[
            pltpu.SemaphoreType.DMA((7,)),
            pltpu.SemaphoreType.DMA((5, fs_count - 1)),
            pltpu.SemaphoreType.DMA((5, fs_count - 1)),
            pltpu.SemaphoreType.DMA((5, pairs - 1)),
            pltpu.SemaphoreType.DMA((5, pairs - 1)),
            pltpu.SemaphoreType.DMA((5, pairs)),
            pltpu.SemaphoreType.DMA((5, pairs)),
        ],
        compiler_params=pltpu.CompilerParams(collective_id=0, has_side_effects=True),
        name="gather_all",
    )(*arrays)


def line_kernel(count, fs_count, whole, *refs):
    sources, landed = refs[:count], refs[count : 2 * count]
    local_sem, sends, recvs = refs[2 * count :]
    dp, fs, _, _, _ = place()
    targets = [lax.rem(fs + o, fs_count) for o in range(1, fs_count)]
    greet([(dp, to) for to in targets])
    copies = [
        push(src if whole else src.at[to], dst.at[fs], sends, recvs, (k, o), (dp, to))
        for k, (src, dst) in enumerate(zip(sources, landed))
        for o, to in enumerate(targets)
    ]
    local = []
    for k, (src, dst) in enumerate(zip(sources, landed)):
        copy = pltpu.make_async_copy(src if whole else src.at[fs], dst.at[fs], local_sem.at[k])
        copy.start()
        local.append(copy)
    for copy in local + copies:
        copy.wait()


def along_line(arrays, whole, collective_id, name):
    fs_count = lax.axis_size("fsdp")
    count = len(arrays)
    return pl.pallas_call(
        functools.partial(line_kernel, count, fs_count, whole),
        out_shape=[
            jax.ShapeDtypeStruct(((fs_count,) + a.shape) if whole else a.shape, a.dtype)
            for a in arrays
        ],
        in_specs=[pl.BlockSpec(memory_space=pltpu.VMEM)] * count,
        out_specs=[pl.BlockSpec(memory_space=pl.ANY)] * count,
        scratch_shapes=[
            pltpu.SemaphoreType.DMA((count,)),
            pltpu.SemaphoreType.DMA((count, fs_count - 1)),
            pltpu.SemaphoreType.DMA((count, fs_count - 1)),
        ],
        compiler_params=pltpu.CompilerParams(collective_id=collective_id, has_side_effects=True),
        name=name,
    )(*arrays)


def whole_sequence(rows, collective_id, name):
    (received,) = along_line([rows], True, collective_id, name)
    return received.reshape(-1, rows.shape[1])


def token_pieces(partial_value):
    fs_count = lax.axis_size("fsdp")
    rows, columns = partial_value.shape
    return partial_value.astype(jnp.bfloat16).reshape(fs_count, rows // fs_count, columns)


def token_share(partial_value, collective_id, name):
    (received,) = along_line([token_pieces(partial_value)], False, collective_id, name)
    return jnp.sum(received.astype(jnp.float32), axis=0)


def token_share_async(partial_value):
    received = lax.all_to_all(
        token_pieces(partial_value), "fsdp", split_axis=0, concat_axis=0, tiled=True
    )
    return jnp.sum(received.astype(jnp.float32), axis=0)


def twin_kernel(count, pairs, *refs):
    partials, received = refs[:count], refs[count : 2 * count]
    sends, recvs = refs[2 * count :]
    _, _, _, core, partner = place()
    greet([partner])
    copies = [
        push(partial.at[j, 1 - core], landed.at[j], sends, recvs, (k, j), partner)
        for k, (partial, landed) in enumerate(zip(partials, received))
        for j in range(pairs)
    ]
    for copy in copies:
        copy.wait()


def pair_kernel(count, pairs, fs_count, *refs):
    partials, pieces = refs[:count], refs[count]
    received, pieces_in = refs[count + 1 : 2 * count + 1], refs[2 * count + 1]
    sends, recvs, z_sends, z_recvs = refs[2 * count + 2 :]
    dp, fs, pair, core, _ = place()
    targets = [lax.rem(pair + o, pairs) for o in range(1, pairs)]
    peers = [(to * CORES + core, fs) for to in targets]
    z_targets = [lax.rem(fs + o, fs_count) for o in range(1, fs_count)]
    greet(peers + [(dp, to) for to in z_targets])
    copies = [
        push(partial.at[to], landed.at[o], sends, recvs, (k, o), peer)
        for k, (partial, landed) in enumerate(zip(partials, received))
        for o, (to, peer) in enumerate(zip(targets, peers))
    ]
    copies += [
        push(pieces.at[to], pieces_in.at[o], z_sends, z_recvs, o, (dp, to))
        for o, to in enumerate(z_targets)
    ]
    for copy in copies:
        copy.wait()


def twin_exchange(partials):
    count = len(partials)
    pairs = lax.axis_size("dp") // CORES
    return pl.pallas_call(
        functools.partial(twin_kernel, count, pairs),
        out_shape=[jax.ShapeDtypeStruct((pairs,) + p.shape[-2:], p.dtype) for p in partials],
        in_specs=[pl.BlockSpec(memory_space=pl.ANY)] * count,
        out_specs=[pl.BlockSpec(memory_space=pl.ANY)] * count,
        scratch_shapes=[pltpu.SemaphoreType.DMA((count, pairs))] * 2,
        compiler_params=pltpu.CompilerParams(collective_id=1, has_side_effects=True),
        name="twin_exchange",
    )(*partials)


def pair_exchange(partials, pieces):
    count = len(partials)
    pairs, fs_count = lax.axis_size("dp") // CORES, lax.axis_size("fsdp")
    slots = [(pairs - 1, p) for p in partials] + [(fs_count - 1, pieces)]
    return pl.pallas_call(
        functools.partial(pair_kernel, count, pairs, fs_count),
        out_shape=[jax.ShapeDtypeStruct((n,) + p.shape[-2:], p.dtype) for n, p in slots],
        in_specs=[pl.BlockSpec(memory_space=pl.ANY)] * len(slots),
        out_specs=[pl.BlockSpec(memory_space=pl.ANY)] * len(slots),
        scratch_shapes=[
            pltpu.SemaphoreType.DMA((count, pairs - 1)),
            pltpu.SemaphoreType.DMA((count, pairs - 1)),
            pltpu.SemaphoreType.DMA((fs_count - 1,)),
            pltpu.SemaphoreType.DMA((fs_count - 1,)),
        ],
        compiler_params=pltpu.CompilerParams(collective_id=2, has_side_effects=True),
        name="pair_exchange",
    )(*partials, pieces)


def reduce_all(partials, pieces):
    dp_count = lax.axis_size("dp")
    pairs = dp_count // CORES
    dp = lax.axis_index("dp")
    core, pair = lax.rem(dp, CORES), dp // CORES
    split = [
        p.reshape(pairs, CORES, p.shape[0] // dp_count, p.shape[1])
        for p in partials
    ]
    landed = twin_exchange(split)
    chip = [
        (
            lax.dynamic_index_in_dim(p, core, axis=1, keepdims=False).astype(jnp.float32)
            + r.astype(jnp.float32)
        ).astype(p.dtype)
        for p, r in zip(split, landed)
    ]
    *others, pieces_in = pair_exchange(chip, pieces)
    own_piece = lax.dynamic_index_in_dim(pieces, lax.axis_index("fsdp"), axis=0, keepdims=False)
    tokens = own_piece.astype(jnp.float32) + jnp.sum(pieces_in.astype(jnp.float32), axis=0)
    return tokens, [
        lax.dynamic_index_in_dim(p, pair, axis=0, keepdims=False).astype(jnp.float32)
        + jnp.sum(r.astype(jnp.float32), axis=0)
        for p, r in zip(chip, others)
    ]


def split_features(
    inputs,
    gain_mixer,
    weight_in,
    conv_taps,
    weight_out,
    gain_ffn,
    weight_gate,
    weight_up,
    weight_down,
    cotangent,
):
    dp_count = lax.axis_size("dp")
    fs_count = lax.axis_size("fsdp")
    width = weight_out.shape[1]
    part = weight_out.shape[0]
    quarter = dp_count * part
    hid = dp_count * weight_down.shape[0]

    small = jnp.concatenate([gain_mixer[None], gain_ffn[None], conv_taps], axis=0)
    lanes = max(128, part)
    small = jnp.pad(small, ((0, 8 - small.shape[0]), (0, lanes - part)))
    gu_blocks = jnp.concatenate(
        [
            column_blocks(weight_gate, 1, dp_count, fs_count),
            column_blocks(weight_up, 1, dp_count, fs_count),
        ],
        axis=2,
    )
    grad_out = cotangent[0]
    x_all, grad_all, small_all, in_cols, gu_cols, out_rows, down_rows = gather_all(
        inputs[0],
        grad_out,
        small,
        column_blocks(weight_in, 3, dp_count, fs_count),
        gu_blocks,
        weight_out,
        weight_down,
    )
    x_all = x_all.reshape(-1, width)
    grad_all = grad_all.reshape(-1, width)
    in_cols = in_cols.reshape(width, 3 * quarter)
    gu_cols = gu_cols.reshape(width, 2 * hid)
    out_rows = out_rows.reshape(quarter, width)
    down_rows = down_rows.reshape(hid, width)
    small_all = small_all[:, :, : KW + 2, :part]
    gain1 = small_all[:, :, 0].reshape(width)
    gain2 = small_all[:, :, 1].reshape(width)
    taps32 = (
        lax.dynamic_index_in_dim(small_all, lax.axis_index("fsdp"), axis=1, keepdims=False)[:, 2:]
        .transpose(1, 0, 2)
        .reshape(KW, quarter)
        .astype(jnp.float32)
    )

    _, _, pre1_all = norm_forward(x_all.astype(jnp.float32), gain1)
    act1_all = pre1_all.astype(jnp.bfloat16)
    projected = product(act1_all, in_cols)
    bpart = projected[:, :quarter]
    cpart = projected[:, quarter : 2 * quarter]
    xpart = projected[:, 2 * quarter :]
    gated = bpart * xpart
    lagged_rows = [lagged(gated, offset) for offset in range(KW)]
    conv = taps32[0] * lagged_rows[0]
    for offset in range(1, KW):
        conv = conv + taps32[offset] * lagged_rows[offset]
    act2 = (cpart * conv).astype(jnp.bfloat16)
    hidden = inputs[0].astype(jnp.float32)
    normed1, scale1, _ = norm_forward(hidden, gain1)
    resid = hidden + token_share(product(act2, out_rows), 3, "share_out")
    normed2, scale2, pre2 = norm_forward(resid, gain2)
    act3_all = whole_sequence(pre2.astype(jnp.bfloat16), 4, "gather_ffn")
    gate_up = product(act3_all, gu_cols)
    gate, upval = gate_up[:, :hid], gate_up[:, hid:]
    sig = jax.nn.sigmoid(gate)
    act4 = (gate * sig * upval).astype(jnp.bfloat16)
    dact4 = product_nt(grad_all, down_rows)
    dgate = (dact4 * upval * sig * (1.0 + gate * (1.0 - sig))).astype(jnp.bfloat16)
    dupval = (dact4 * gate * sig).astype(jnp.bfloat16)
    dgu = jnp.concatenate([dgate, dupval], axis=1)
    dact3 = token_share(product_nt(dgu, gu_cols), 5, "share_ffn")
    down_pieces = token_pieces(product(act4, down_rows))
    dnorm2, g_gain2 = norm_backward(dact3, normed2, scale2, gain2)
    dresid = grad_out.astype(jnp.float32) + dnorm2
    dres_all = whole_sequence(dresid.astype(jnp.bfloat16), 6, "gather_dres")
    dact2 = product_nt(dres_all, out_rows)
    dcpart = dact2 * conv
    dconv = dact2 * cpart
    g_taps = jnp.stack(
        [jnp.sum(dconv * lagged_rows[offset], axis=0) for offset in range(KW)], axis=0
    )
    dgated = taps32[0] * dconv
    for offset in range(1, KW):
        dgated = dgated + taps32[offset] * leading(dconv, offset)
    dproj = jnp.concatenate([dgated * xpart, dcpart, dgated * bpart], axis=1).astype(jnp.bfloat16)
    dact1 = token_share_async(product_nt(dproj, in_cols))
    dnorm1, g_gain1 = norm_backward(dact1, normed1, scale1, gain1)
    grad_inputs = dresid + dnorm1

    own_column = (jnp.arange(fs_count) == lax.axis_index("fsdp"))[None, None, :, None]
    taps_spread = jnp.where(own_column, g_taps.reshape(KW, dp_count, 1, part), 0.0).reshape(KW, width)
    small_grad = jnp.concatenate([g_gain1[None], g_gain2[None], taps_spread], axis=0)
    small_grad = jnp.pad(small_grad, ((0, 8 - small_grad.shape[0]), (0, 0)))
    small_grad = small_grad.reshape(8, dp_count, fs_count, part).transpose(1, 2, 0, 3)
    small_grad = jnp.pad(small_grad, ((0, 0), (0, 0), (0, 0), (0, lanes - part)))
    down_sum, (g_small, g_gu, g_down, g_in, g_out) = reduce_all(
        [small_grad.reshape(dp_count * fs_count * 8, lanes)]
        + [
            grad.astype(jnp.bfloat16)
            for grad in (
                product_tn(act3_all, dgu),
                product_tn(act4, grad_all),
                product_tn(act1_all, dproj),
                product_tn(act2, dres_all),
            )
        ],
        down_pieces,
    )
    outputs = (resid + down_sum).astype(jnp.bfloat16)
    moved = jnp.concatenate([g_in, g_gu], axis=1).astype(jnp.bfloat16)
    moved, small_parts = along_line(
        [
            moved.reshape(fs_count, part, 3 * quarter + 2 * hid),
            g_small.reshape(fs_count, 8, lanes),
        ],
        False,
        7,
        "owner_exchange",
    )
    moved = moved.astype(jnp.float32)
    g_in_owned = moved[:, :, : 3 * quarter]
    g_gu_owned = moved[:, :, 3 * quarter :]
    small_owned = jnp.sum(small_parts, axis=0)[: KW + 2, :part]
    return (
        outputs[None],
        grad_inputs[None],
        small_owned[0],
        column_join(g_in_owned, 3, dp_count, fs_count),
        small_owned[2:],
        g_out,
        small_owned[1],
        column_join(g_gu_owned[:, :, :hid], 1, dp_count, fs_count),
        column_join(g_gu_owned[:, :, hid:], 1, dp_count, fs_count),
        g_down,
    )


def on_device(
    inputs,
    gain_mixer,
    weight_in,
    conv_taps,
    weight_out,
    gain_ffn,
    weight_gate,
    weight_up,
    weight_down,
    cotangent,
):
    return split_features(
        inputs,
        gain_mixer,
        weight_in,
        conv_taps,
        weight_out,
        gain_ffn,
        weight_gate,
        weight_up,
        weight_down,
        cotangent,
    )


def solution(mesh):
    in_specs = (
        P("dp", "fsdp", None),
        P(("dp", "fsdp")),
        P(("dp", "fsdp"), None),
        P(None, ("dp", "fsdp")),
        P(("dp", "fsdp"), None),
        P(("dp", "fsdp")),
        P(("dp", "fsdp"), None),
        P(("dp", "fsdp"), None),
        P(("dp", "fsdp"), None),
        P("dp", "fsdp", None),
    )
    out_specs = (
        P("dp", "fsdp", None),
        P("dp", "fsdp", None),
        P(("dp", "fsdp")),
        P(("dp", "fsdp"), None),
        P(None, ("dp", "fsdp")),
        P(("dp", "fsdp"), None),
        P(("dp", "fsdp")),
        P(("dp", "fsdp"), None),
        P(("dp", "fsdp"), None),
        P(("dp", "fsdp"), None),
    )
    return jax.shard_map(
        on_device, mesh=mesh, in_specs=in_specs, out_specs=out_specs, check_vma=False
    )
```

```python
import functools

import jax
import jax.numpy as jnp
from jax import lax
from jax.experimental import pallas as pl
from jax.experimental.pallas import tpu as pltpu
from jax.sharding import PartitionSpec as P

KW = 3


EPS = 1e-05

CORES = 2
MESH = pl.DeviceIdType.MESH


def product(left, right):
    return jnp.dot(left, right, preferred_element_type=jnp.float32)


def product_tn(left, right):
    return lax.dot_general(
        left, right, (((0,), (0,)), ((), ())), preferred_element_type=jnp.float32
    )


def product_nt(left, right):
    return lax.dot_general(
        left, right, (((1,), (1,)), ((), ())), preferred_element_type=jnp.float32
    )


def norm_forward(hidden, gain):
    scale = lax.rsqrt(jnp.mean(hidden * hidden, axis=-1, keepdims=True) + EPS)
    normed = hidden * scale
    return (normed, scale, normed * gain.astype(jnp.float32))


def norm_backward(dact, normed, scale, gain):
    dnormed = dact * gain.astype(jnp.float32)
    dhidden = scale * (dnormed - normed * jnp.mean(dnormed * normed, axis=-1, keepdims=True))
    return (dhidden, jnp.sum(dact * normed, axis=0))


def lagged(values, offset):
    zeros = jnp.zeros((offset, values.shape[1]), values.dtype)
    return jnp.concatenate([zeros, values[: values.shape[0] - offset]], axis=0)


def leading(values, offset):
    zeros = jnp.zeros((offset, values.shape[1]), values.dtype)
    return jnp.concatenate([values[offset:], zeros], axis=0)


def column_blocks(shard, lead, dp_count, fs_count):
    rows, columns = shard.shape
    inner = columns // (lead * dp_count * fs_count)
    pieces = shard.reshape(rows, lead, dp_count, fs_count, inner).transpose(3, 0, 1, 2, 4)
    return pieces.reshape(fs_count, rows, lead * dp_count * inner)


def column_join(blocks, lead, dp_count, fs_count):
    _, rows, columns = blocks.shape
    inner = columns // (lead * dp_count)
    pieces = blocks.reshape(fs_count, rows, lead, dp_count, inner).transpose(1, 2, 3, 0, 4)
    return pieces.reshape(rows, lead * dp_count * fs_count * inner)


def greet(peers):
    barrier = pltpu.get_barrier_semaphore()
    for peer in peers:
        pl.semaphore_signal(barrier, inc=1, device_id=peer, device_id_type=MESH)
    pl.semaphore_wait(barrier, len(peers))


def push(src, dst, sends, recvs, index, peer):
    copy = pltpu.make_async_remote_copy(
        src_ref=src,
        dst_ref=dst,
        send_sem=sends.at[index],
        recv_sem=recvs.at[index],
        device_id=peer,
        device_id_type=MESH,
    )
    copy.start()
    return copy


def place():
    dp, fs = lax.axis_index("dp"), lax.axis_index("fsdp")
    pair, core = dp // CORES, lax.rem(dp, CORES)
    return dp, fs, pair, core, (pair * CORES + 1 - core, fs)


def gather_kernel(
    pairs, fs_count,
    x_ref, cot_ref, small_ref, in_ref, gu_ref, out_ref, down_ref,
    x_all, cot_all, small_all, in_all, gu_all, out_all, down_all,
    local_sem, z_send, z_recv, p_send, p_recv, c_send, c_recv,
):
    dp, fs, pair, core, partner = place()
    z_peers = [(dp, lax.rem(fs + o, fs_count)) for o in range(1, fs_count)]
    p_peers = [(lax.rem(pair + o, pairs) * CORES + core, fs) for o in range(1, pairs)]
    p_from = [lax.rem(pair + pairs - o, pairs) * CORES + core for o in range(1, pairs)]
    greet(z_peers + p_peers + [partner])
    spread = [small_all, in_all, gu_all, out_all, down_all]

    across = [[None] * len(p_peers) for _ in spread]
    twins = [[None] * pairs for _ in spread]

    def spread_own(kind, src):
        dst = spread[kind].at[dp]
        for o, peer in enumerate(p_peers):
            across[kind][o] = push(src, dst, p_send, p_recv, (kind, o), peer)
        twins[kind][0] = push(src, dst, c_send, c_recv, (kind, 0), partner)

    along = [[], [], [], [], []]
    for o, peer in enumerate(z_peers):
        to = peer[1]
        along[0].append(push(small_ref, small_all.at[dp, fs], z_send, z_recv, (0, o), peer))
        along[1].append(push(in_ref.at[to], in_all.at[dp, fs], z_send, z_recv, (1, o), peer))
    for o, peer in enumerate(z_peers):
        to = peer[1]
        along[2].append(push(gu_ref.at[to], gu_all.at[dp, fs], z_send, z_recv, (2, o), peer))
    for o, peer in enumerate(z_peers):
        along[3].append(push(x_ref, x_all.at[fs], z_send, z_recv, (3, o), peer))
    for o, peer in enumerate(z_peers):
        along[4].append(push(cot_ref, cot_all.at[fs], z_send, z_recv, (4, o), peer))
    spread_own(3, out_ref)
    spread_own(4, down_ref)
    local = []
    for index, (src, dst) in enumerate(
        [
            (small_ref, small_all.at[dp, fs]),
            (in_ref.at[fs], in_all.at[dp, fs]),
            (gu_ref.at[fs], gu_all.at[dp, fs]),
            (x_ref, x_all.at[fs]),
            (cot_ref, cot_all.at[fs]),
            (out_ref, out_all.at[dp]),
            (down_ref, down_all.at[dp]),
        ]
    ):
        copy = pltpu.make_async_copy(src, dst, local_sem.at[index])
        copy.start()
        local.append(copy)
    for kind in range(3):
        local[kind].wait()
        for copy in along[kind]:
            copy.wait_recv()
        spread_own(kind, spread[kind].at[dp])
    for kind in (3, 0, 1, 4, 2):
        for o, source in enumerate(p_from):
            across[kind][o].wait_recv()
            block = spread[kind].at[source]
            twins[kind][o + 1] = push(block, block, c_send, c_recv, (kind, o + 1), partner)
    for copy in local[3:]:
        copy.wait()
    for copy in along[3] + along[4]:
        copy.wait_recv()
    for row in along + across:
        for copy in row:
            copy.wait_send()
    for row in twins:
        for copy in row:
            copy.wait()


def gather_all(x, cot, small, in_blocks, gu_blocks, out_shard, down_shard):
    dp_count, fs_count = lax.axis_size("dp"), lax.axis_size("fsdp")
    pairs = dp_count // CORES
    arrays = (x, cot, small, in_blocks, gu_blocks, out_shard, down_shard)
    shapes = (
        (fs_count,) + x.shape,
        (fs_count,) + cot.shape,
        (dp_count, fs_count) + small.shape,
        (dp_count,) + in_blocks.shape,
        (dp_count,) + gu_blocks.shape,
        (dp_count,) + out_shard.shape,
        (dp_count,) + down_shard.shape,
    )
    return pl.pallas_call(
        functools.partial(gather_kernel, pairs, fs_count),
        out_shape=[jax.ShapeDtypeStruct(shape, x.dtype) for shape in shapes],
        in_specs=[pl.BlockSpec(memory_space=pltpu.VMEM)] * len(arrays),
        out_specs=[pl.BlockSpec(memory_space=pl.ANY)] * len(shapes),
        scratch_shapes=[
            pltpu.SemaphoreType.DMA((7,)),
            pltpu.SemaphoreType.DMA((5, fs_count - 1)),
            pltpu.SemaphoreType.DMA((5, fs_count - 1)),
            pltpu.SemaphoreType.DMA((5, pairs - 1)),
            pltpu.SemaphoreType.DMA((5, pairs - 1)),
            pltpu.SemaphoreType.DMA((5, pairs)),
            pltpu.SemaphoreType.DMA((5, pairs)),
        ],
        compiler_params=pltpu.CompilerParams(collective_id=0, has_side_effects=True),
        name="gather_all",
    )(*arrays)


def line_kernel(count, fs_count, whole, *refs):
    sources, landed = refs[:count], refs[count : 2 * count]
    local_sem, sends, recvs = refs[2 * count :]
    dp, fs, _, _, _ = place()
    targets = [lax.rem(fs + o, fs_count) for o in range(1, fs_count)]
    greet([(dp, to) for to in targets])
    copies = [
        push(src if whole else src.at[to], dst.at[fs], sends, recvs, (k, o), (dp, to))
        for k, (src, dst) in enumerate(zip(sources, landed))
        for o, to in enumerate(targets)
    ]
    local = []
    for k, (src, dst) in enumerate(zip(sources, landed)):
        copy = pltpu.make_async_copy(src if whole else src.at[fs], dst.at[fs], local_sem.at[k])
        copy.start()
        local.append(copy)
    for copy in local + copies:
        copy.wait()


def along_line(arrays, whole, collective_id, name):
    fs_count = lax.axis_size("fsdp")
    count = len(arrays)
    return pl.pallas_call(
        functools.partial(line_kernel, count, fs_count, whole),
        out_shape=[
            jax.ShapeDtypeStruct(((fs_count,) + a.shape) if whole else a.shape, a.dtype)
            for a in arrays
        ],
        in_specs=[pl.BlockSpec(memory_space=pltpu.VMEM)] * count,
        out_specs=[pl.BlockSpec(memory_space=pl.ANY)] * count,
        scratch_shapes=[
            pltpu.SemaphoreType.DMA((count,)),
            pltpu.SemaphoreType.DMA((count, fs_count - 1)),
            pltpu.SemaphoreType.DMA((count, fs_count - 1)),
        ],
        compiler_params=pltpu.CompilerParams(collective_id=collective_id, has_side_effects=True),
        name=name,
    )(*arrays)


def whole_sequence(rows, collective_id, name):
    (received,) = along_line([rows], True, collective_id, name)
    return received.reshape(-1, rows.shape[1])


def token_pieces(partial_value):
    fs_count = lax.axis_size("fsdp")
    rows, columns = partial_value.shape
    return partial_value.astype(jnp.bfloat16).reshape(fs_count, rows // fs_count, columns)


def token_share(partial_value, collective_id, name):
    (received,) = along_line([token_pieces(partial_value)], False, collective_id, name)
    return jnp.sum(received.astype(jnp.float32), axis=0)


def token_share_async(partial_value):
    received = lax.all_to_all(
        token_pieces(partial_value), "fsdp", split_axis=0, concat_axis=0, tiled=True
    )
    return jnp.sum(received.astype(jnp.float32), axis=0)


def twin_kernel(count, pairs, *refs):
    partials, received = refs[:count], refs[count : 2 * count]
    sends, recvs = refs[2 * count :]
    _, _, _, core, partner = place()
    greet([partner])
    copies = [
        push(partial.at[j, 1 - core], landed.at[j], sends, recvs, (k, j), partner)
        for k, (partial, landed) in enumerate(zip(partials, received))
        for j in range(pairs)
    ]
    for copy in copies:
        copy.wait()


def pair_kernel(count, pairs, fs_count, *refs):
    partials, pieces = refs[:count], refs[count]
    received, pieces_in = refs[count + 1 : 2 * count + 1], refs[2 * count + 1]
    sends, recvs, z_sends, z_recvs = refs[2 * count + 2 :]
    dp, fs, pair, core, _ = place()
    targets = [lax.rem(pair + o, pairs) for o in range(1, pairs)]
    peers = [(to * CORES + core, fs) for to in targets]
    z_targets = [lax.rem(fs + o, fs_count) for o in range(1, fs_count)]
    greet(peers + [(dp, to) for to in z_targets])
    copies = [
        push(partial.at[to], landed.at[o], sends, recvs, (k, o), peer)
        for k, (partial, landed) in enumerate(zip(partials, received))
        for o, (to, peer) in enumerate(zip(targets, peers))
    ]
    copies += [
        push(pieces.at[to], pieces_in.at[o], z_sends, z_recvs, o, (dp, to))
        for o, to in enumerate(z_targets)
    ]
    for copy in copies:
        copy.wait()


def twin_exchange(partials, collective_id, name):
    count = len(partials)
    pairs = lax.axis_size("dp") // CORES
    return pl.pallas_call(
        functools.partial(twin_kernel, count, pairs),
        out_shape=[jax.ShapeDtypeStruct((pairs,) + p.shape[-2:], p.dtype) for p in partials],
        in_specs=[pl.BlockSpec(memory_space=pl.ANY)] * count,
        out_specs=[pl.BlockSpec(memory_space=pl.ANY)] * count,
        scratch_shapes=[pltpu.SemaphoreType.DMA((count, pairs))] * 2,
        compiler_params=pltpu.CompilerParams(collective_id=collective_id, has_side_effects=True),
        name=name,
    )(*partials)


def pair_exchange(partials, pieces, collective_id, name):
    count = len(partials)
    pairs, fs_count = lax.axis_size("dp") // CORES, lax.axis_size("fsdp")
    slots = [(pairs - 1, p) for p in partials] + [(fs_count - 1, pieces)]
    return pl.pallas_call(
        functools.partial(pair_kernel, count, pairs, fs_count),
        out_shape=[jax.ShapeDtypeStruct((n,) + p.shape[-2:], p.dtype) for n, p in slots],
        in_specs=[pl.BlockSpec(memory_space=pl.ANY)] * len(slots),
        out_specs=[pl.BlockSpec(memory_space=pl.ANY)] * len(slots),
        scratch_shapes=[
            pltpu.SemaphoreType.DMA((count, pairs - 1)),
            pltpu.SemaphoreType.DMA((count, pairs - 1)),
            pltpu.SemaphoreType.DMA((fs_count - 1,)),
            pltpu.SemaphoreType.DMA((fs_count - 1,)),
        ],
        compiler_params=pltpu.CompilerParams(collective_id=collective_id, has_side_effects=True),
        name=name,
    )(*partials, pieces)


def reduce_all(partials, pieces, ids, label):
    dp_count = lax.axis_size("dp")
    pairs = dp_count // CORES
    dp = lax.axis_index("dp")
    core, pair = lax.rem(dp, CORES), dp // CORES
    split = [
        p.reshape(pairs, CORES, p.shape[0] // dp_count, p.shape[1])
        for p in partials
    ]
    landed = twin_exchange(split, ids[0], "twin_" + label)
    chip = [
        (
            lax.dynamic_index_in_dim(p, core, axis=1, keepdims=False).astype(jnp.float32)
            + r.astype(jnp.float32)
        ).astype(p.dtype)
        for p, r in zip(split, landed)
    ]
    *others, pieces_in = pair_exchange(chip, pieces, ids[1], "pair_" + label)
    own_piece = lax.dynamic_index_in_dim(pieces, lax.axis_index("fsdp"), axis=0, keepdims=False)
    tokens = own_piece.astype(jnp.float32) + jnp.sum(pieces_in.astype(jnp.float32), axis=0)
    return tokens, [
        lax.dynamic_index_in_dim(p, pair, axis=0, keepdims=False).astype(jnp.float32)
        + jnp.sum(r.astype(jnp.float32), axis=0)
        for p, r in zip(chip, others)
    ]


def split_features(
    inputs,
    gain_mixer,
    weight_in,
    conv_taps,
    weight_out,
    gain_ffn,
    weight_gate,
    weight_up,
    weight_down,
    cotangent,
):
    dp_count = lax.axis_size("dp")
    fs_count = lax.axis_size("fsdp")
    width = weight_out.shape[1]
    part = weight_out.shape[0]
    quarter = dp_count * part
    hid = dp_count * weight_down.shape[0]

    small = jnp.concatenate([gain_mixer[None], gain_ffn[None], conv_taps], axis=0)
    lanes = max(128, part)
    small = jnp.pad(small, ((0, 8 - small.shape[0]), (0, lanes - part)))
    gu_blocks = jnp.concatenate(
        [
            column_blocks(weight_gate, 1, dp_count, fs_count),
            column_blocks(weight_up, 1, dp_count, fs_count),
        ],
        axis=2,
    )
    grad_out = cotangent[0]
    x_all, grad_all, small_all, in_cols, gu_cols, out_rows, down_rows = gather_all(
        inputs[0],
        grad_out,
        small,
        column_blocks(weight_in, 3, dp_count, fs_count),
        gu_blocks,
        weight_out,
        weight_down,
    )
    x_all = x_all.reshape(-1, width)
    grad_all = grad_all.reshape(-1, width)
    in_cols = in_cols.reshape(width, 3 * quarter)
    gu_cols = gu_cols.reshape(width, 2 * hid)
    out_rows = out_rows.reshape(quarter, width)
    down_rows = down_rows.reshape(hid, width)
    small_all = small_all[:, :, : KW + 2, :part]
    gain1 = small_all[:, :, 0].reshape(width)
    gain2 = small_all[:, :, 1].reshape(width)
    taps32 = (
        lax.dynamic_index_in_dim(small_all, lax.axis_index("fsdp"), axis=1, keepdims=False)[:, 2:]
        .transpose(1, 0, 2)
        .reshape(KW, quarter)
        .astype(jnp.float32)
    )

    _, _, pre1_all = norm_forward(x_all.astype(jnp.float32), gain1)
    act1_all = pre1_all.astype(jnp.bfloat16)
    projected = product(act1_all, in_cols)
    bpart = projected[:, :quarter]
    cpart = projected[:, quarter : 2 * quarter]
    xpart = projected[:, 2 * quarter :]
    gated = bpart * xpart
    lagged_rows = [lagged(gated, offset) for offset in range(KW)]
    conv = taps32[0] * lagged_rows[0]
    for offset in range(1, KW):
        conv = conv + taps32[offset] * lagged_rows[offset]
    act2 = (cpart * conv).astype(jnp.bfloat16)
    hidden = inputs[0].astype(jnp.float32)
    normed1, scale1, _ = norm_forward(hidden, gain1)
    resid = hidden + token_share(product(act2, out_rows), 3, "share_out")
    normed2, scale2, pre2 = norm_forward(resid, gain2)
    act3_all = whole_sequence(pre2.astype(jnp.bfloat16), 4, "gather_ffn")
    gate_up = product(act3_all, gu_cols)
    gate, upval = gate_up[:, :hid], gate_up[:, hid:]
    sig = jax.nn.sigmoid(gate)
    act4 = (gate * sig * upval).astype(jnp.bfloat16)
    dact4 = product_nt(grad_all, down_rows)
    dgate = (dact4 * upval * sig * (1.0 + gate * (1.0 - sig))).astype(jnp.bfloat16)
    dupval = (dact4 * gate * sig).astype(jnp.bfloat16)
    dgu = jnp.concatenate([dgate, dupval], axis=1)
    dact3, (g_gu, g_down) = reduce_all(
        [
            product_tn(act3_all, dgu).astype(jnp.bfloat16),
            product_tn(act4, grad_all).astype(jnp.bfloat16),
        ],
        token_pieces(product_nt(dgu, gu_cols)),
        (1, 2),
        "ffn",
    )
    down_pieces = token_pieces(product(act4, down_rows))
    dnorm2, g_gain2 = norm_backward(dact3, normed2, scale2, gain2)
    dresid = grad_out.astype(jnp.float32) + dnorm2
    dres_all = whole_sequence(dresid.astype(jnp.bfloat16), 6, "gather_dres")
    dact2 = product_nt(dres_all, out_rows)
    dcpart = dact2 * conv
    dconv = dact2 * cpart
    g_taps = jnp.stack(
        [jnp.sum(dconv * lagged_rows[offset], axis=0) for offset in range(KW)], axis=0
    )
    dgated = taps32[0] * dconv
    for offset in range(1, KW):
        dgated = dgated + taps32[offset] * leading(dconv, offset)
    dproj = jnp.concatenate([dgated * xpart, dcpart, dgated * bpart], axis=1).astype(jnp.bfloat16)
    dact1 = token_share_async(product_nt(dproj, in_cols))
    dnorm1, g_gain1 = norm_backward(dact1, normed1, scale1, gain1)
    grad_inputs = dresid + dnorm1

    own_column = (jnp.arange(fs_count) == lax.axis_index("fsdp"))[None, None, :, None]
    taps_spread = jnp.where(own_column, g_taps.reshape(KW, dp_count, 1, part), 0.0).reshape(KW, width)
    small_grad = jnp.concatenate([g_gain1[None], g_gain2[None], taps_spread], axis=0)
    small_grad = jnp.pad(small_grad, ((0, 8 - small_grad.shape[0]), (0, 0)))
    small_grad = small_grad.reshape(8, dp_count, fs_count, part).transpose(1, 2, 0, 3)
    small_grad = jnp.pad(small_grad, ((0, 0), (0, 0), (0, 0), (0, lanes - part)))
    down_sum, (g_small, g_in, g_out) = reduce_all(
        [small_grad.reshape(dp_count * fs_count * 8, lanes)]
        + [
            grad.astype(jnp.bfloat16)
            for grad in (
                product_tn(act1_all, dproj),
                product_tn(act2, dres_all),
            )
        ],
        down_pieces,
        (5, 8),
        "mixer",
    )
    outputs = (resid + down_sum).astype(jnp.bfloat16)
    moved = jnp.concatenate([g_in, g_gu], axis=1).astype(jnp.bfloat16)
    moved, small_parts = along_line(
        [
            moved.reshape(fs_count, part, 3 * quarter + 2 * hid),
            g_small.reshape(fs_count, 8, lanes),
        ],
        False,
        7,
        "owner_exchange",
    )
    moved = moved.astype(jnp.float32)
    g_in_owned = moved[:, :, : 3 * quarter]
    g_gu_owned = moved[:, :, 3 * quarter :]
    small_owned = jnp.sum(small_parts, axis=0)[: KW + 2, :part]
    return (
        outputs[None],
        grad_inputs[None],
        small_owned[0],
        column_join(g_in_owned, 3, dp_count, fs_count),
        small_owned[2:],
        g_out,
        small_owned[1],
        column_join(g_gu_owned[:, :, :hid], 1, dp_count, fs_count),
        column_join(g_gu_owned[:, :, hid:], 1, dp_count, fs_count),
        g_down,
    )


def on_device(
    inputs,
    gain_mixer,
    weight_in,
    conv_taps,
    weight_out,
    gain_ffn,
    weight_gate,
    weight_up,
    weight_down,
    cotangent,
):
    return split_features(
        inputs,
        gain_mixer,
        weight_in,
        conv_taps,
        weight_out,
        gain_ffn,
        weight_gate,
        weight_up,
        weight_down,
        cotangent,
    )


def solution(mesh):
    in_specs = (
        P("dp", "fsdp", None),
        P(("dp", "fsdp")),
        P(("dp", "fsdp"), None),
        P(None, ("dp", "fsdp")),
        P(("dp", "fsdp"), None),
        P(("dp", "fsdp")),
        P(("dp", "fsdp"), None),
        P(("dp", "fsdp"), None),
        P(("dp", "fsdp"), None),
        P("dp", "fsdp", None),
    )
    out_specs = (
        P("dp", "fsdp", None),
        P("dp", "fsdp", None),
        P(("dp", "fsdp")),
        P(("dp", "fsdp"), None),
        P(None, ("dp", "fsdp")),
        P(("dp", "fsdp"), None),
        P(("dp", "fsdp")),
        P(("dp", "fsdp"), None),
        P(("dp", "fsdp"), None),
        P(("dp", "fsdp"), None),
    )
    return jax.shard_map(
        on_device, mesh=mesh, in_specs=in_specs, out_specs=out_specs, check_vma=False
    )
```
